256 devices in a mesh: af: 64 (over y_hi, z, x), row: 4 (over y_lo, core).
Axes of the slice: x: 4, y: 4 (y_hi: 2, y_lo: 2; y = y_hi * 2 + y_lo), z: 8, core: 2. Of those that a mesh axis runs over, the one named last changes fastest.
Arguments:
- source_traces: bfloat16 [512, 1024, 2048], P('af', 'row'), may hold values from -6 to 6
- receiver_traces: bfloat16 [128, 1024, 2048], P('row', 'af'), may hold values from -6 to 6
- wavelet_inverse: float32 [64, 2], replicated, may hold values from -4 to 4
Outputs:
- multiples: bfloat16 [512, 128, 2048], P('af', 'row')
The draws below stay inside these ranges and needn't reach their ends.
All inputs are finite; a program needn't handle non-finite values.
Results may differ from the reference program's by a relative error of at most 0.008.
Values may be sent and summed in bfloat16 or wider, within the bound.
No kernel may reach another device: no remote copies, remote signals or barrier semaphores. Data moves between devices by JAX's collectives and lax.ppermute only.
A program may use at most 64 MiB of HBM per device.

```python
import math
import jax
import jax.numpy as jnp
from jax import lax

NT = 2048
NF = 64
F_LOW = 96
K = 1024
S = 512
R = 128


def shard_levels(own_key, dims, shards, smallest, top_value):
    loudness = 1.0
    for dim, blocks in shards:
        heights = jax.random.uniform(jax.random.fold_in(jax.random.fold_in(own_key, 6), dim), (blocks,), jnp.float32, smallest / len(shards), top_value / len(shards))
        loudness = loudness * jnp.repeat(jnp.exp(heights), dims[dim] // blocks).reshape((-1,) + (1,) * (len(dims) - 1 - dim))
    return loudness


def noise(key, dims, scale, bound, cuts=(), held_as=jnp.bfloat16):
    loudness = shard_levels(key, dims, cuts, -0.22, 0.18) if cuts else 1.0
    values = jax.random.normal(key, dims, jnp.float32) * scale * loudness
    return jnp.minimum(jnp.maximum(values, -bound), bound).astype(held_as)


def setup_inputs(seed: int = 0) -> dict:
    splits = jax.random.split(jax.random.key(seed), 4)
    source_traces = noise(splits[0], (S, K, NT), 1.0, 6.0, ((0, 64), (1, 4)))
    receiver_traces = noise(splits[1], (R, K, NT), 1.0, 6.0, ((0, 4), (1, 64)))
    wavelet_inverse = noise(splits[2], (NF, 2), 1.0, 4.0, (), jnp.float32)
    return dict(source_traces=source_traces, receiver_traces=receiver_traces, wavelet_inverse=wavelet_inverse)


def tables(amplitude):
    samples = jnp.arange(NT, dtype=jnp.int32)
    frequency = F_LOW + jnp.arange(NF, dtype=jnp.int32)
    phase_index = frequency[:, None] * samples[None, :] % NT
    angles = phase_index.astype(jnp.float32) * (2.0 * math.pi / NT)
    return jnp.stack([jnp.cos(angles) * amplitude, -jnp.sin(angles) * amplitude], axis=1).astype(jnp.bfloat16)

def reference(source_traces, receiver_traces, wavelet_inverse):
    forward = tables(1.0 / math.sqrt(NT))
    forward_mat = forward.reshape(2 * NF, NT).T.astype(jnp.float32)

    def spectrum(traces):
        return jnp.dot(traces.astype(jnp.float32), forward_mat).astype(jnp.bfloat16)
    source_spec = lax.map(spectrum, source_traces).reshape(S, K, NF, 2)
    receiver_spec = lax.map(spectrum, receiver_traces).reshape(R, K, NF, 2)
    amplitude = 1.0 / math.sqrt(K)

    def one_freq(freq_index):
        source_one = lax.dynamic_index_in_dim(source_spec, freq_index, 2, keepdims=False).astype(jnp.float32)
        receiver_one = lax.dynamic_index_in_dim(receiver_spec, freq_index, 2, keepdims=False).astype(jnp.float32)
        src_real = source_one[:, :, 0]
        src_imag = source_one[:, :, 1]
        rcv_real = receiver_one[:, :, 0].T
        rcv_imag = receiver_one[:, :, 1].T
        raw_real = jnp.dot(src_real, rcv_real) - jnp.dot(src_imag, rcv_imag)
        raw_imag = jnp.dot(src_real, rcv_imag) + jnp.dot(src_imag, rcv_real)
        wave_pair = lax.dynamic_index_in_dim(wavelet_inverse, freq_index, 0, keepdims=False)
        pred_real = (raw_real * wave_pair[0] - raw_imag * wave_pair[1]) * amplitude
        pred_imag = (raw_real * wave_pair[1] + raw_imag * wave_pair[0]) * amplitude
        return jnp.stack([pred_real, pred_imag], axis=0).astype(jnp.bfloat16)
    predicted = lax.map(one_freq, jnp.arange(NF, dtype=jnp.int32))
    inverse = tables(1.0 / math.sqrt(NF)).reshape(2 * NF, NT).astype(jnp.float32)
    columns = predicted.reshape(2 * NF, S * R).T.astype(jnp.float32)
    result = jnp.dot(columns, inverse)
    return result.reshape(S, R, NT).astype(jnp.bfloat16)
```

```python
import math

import jax
import jax.numpy as jnp
import numpy as np
from jax import lax
from jax.sharding import Mesh, PartitionSpec as P

NT = 2048
NF = 64
F_LOW = 96
K = 1024

AXES = ("yh", "z1", "z0", "x", "yl", "core")
AF = ("yh", "z1", "z0", "x")
ROW = ("yl", "core")
GROUP = ("yh", "z0", "x", "yl", "core")


def tables(amplitude):
    samples = np.arange(NT, dtype=np.int64)
    frequency = F_LOW + np.arange(NF, dtype=np.int64)
    phase_index = frequency[:, None] * samples[None, :] % NT
    angles = phase_index.astype(np.float64) * (2.0 * math.pi / NT)
    return np.stack([np.cos(angles), -np.sin(angles)], axis=1) * amplitude


def per_device(source_traces, receiver_traces, wavelet_inverse):
    forward = jnp.asarray(tables(1.0 / math.sqrt(NT)), jnp.bfloat16)
    receiver_spec = jnp.einsum(
        "fct,rkt->fckr", forward, receiver_traces, preferred_element_type=jnp.float32
    ).astype(jnp.bfloat16)
    receiver_spec = receiver_spec.reshape(NF, -1)
    other = [
        lax.ppermute(receiver_spec, "z1", [(i, (i + hop) % 4) for i in range(4)])
        for hop in (2, 1, 3)
    ]
    source_spec = (
        jnp.einsum("fct,skt->fcsk", forward, source_traces, preferred_element_type=jnp.float32)
        .astype(jnp.bfloat16)
        .reshape(NF, -1)
    )
    sent = jnp.concatenate([source_spec, receiver_spec] + other, axis=1)
    got = lax.all_to_all(sent, GROUP, split_axis=0, concat_axis=0, tiled=True)
    n_src = 2 * 8 * 256
    source_freq = got[:, :n_src].reshape(2, 2, 4, 4, 2, 8, 256)
    source_freq = source_freq.transpose(4, 0, 1, 2, 5, 3, 6).reshape(2, 128, K)
    receiver_freq = got[:, n_src:].reshape(2, 2, 4, 4, 4, 2, 16, 32)
    own = lax.axis_index("z1")
    slots = jnp.array([0, 2, 1, 3], jnp.int32)
    order = slots[(own - jnp.arange(4)) % 4]
    receiver_freq = receiver_freq.transpose(4, 5, 0, 1, 2, 6, 3, 7)
    receiver_freq = jnp.take(receiver_freq, order, axis=0)
    receiver_freq = receiver_freq.transpose(1, 2, 0, 3, 4, 5, 6, 7).reshape(2, K, 128)
    real, imag = receiver_freq[0], receiver_freq[1]
    coupled = jnp.concatenate(
        [jnp.concatenate([real, imag], axis=1), jnp.concatenate([-imag, real], axis=1)], axis=0
    )
    raw = jnp.einsum(
        "sk,kr->sr",
        jnp.concatenate([source_freq[0], source_freq[1]], axis=1),
        coupled,
        preferred_element_type=jnp.float32,
    )
    raw_real, raw_imag = raw[:, :128], raw[:, 128:]
    wavelet = lax.dynamic_slice_in_dim(wavelet_inverse, lax.axis_index(GROUP), 1, 0)
    wave_real, wave_imag = wavelet[0, 0], wavelet[0, 1]
    amplitude = 1.0 / math.sqrt(K)
    pred_real = (raw_real * wave_real - raw_imag * wave_imag) * amplitude
    pred_imag = (raw_real * wave_imag + raw_imag * wave_real) * amplitude
    predicted = jnp.stack([pred_real, pred_imag]).astype(jnp.bfloat16)
    predicted = predicted.reshape(2, 16, 8, 4, 32).transpose(1, 3, 0, 2, 4).reshape(NF, 2, 256)
    returned = lax.all_to_all(predicted, GROUP, split_axis=0, concat_axis=0, tiled=True)
    inverse = jnp.asarray(tables(1.0 / math.sqrt(NF)), jnp.bfloat16)
    result = jnp.einsum("fcm,fct->mt", returned, inverse, preferred_element_type=jnp.float32)
    return result.astype(jnp.bfloat16).reshape(8, 32, NT)


def solution(mesh):
    fine = Mesh(np.asarray(mesh.devices).reshape(2, 4, 2, 4, 2, 2), AXES)
    return jax.shard_map(
        per_device,
        mesh=fine,
        in_specs=(P(AF, ROW, None), P(ROW, AF, None), P()),
        out_specs=P(AF, ROW, None),
        check_vma=False,
    )
```

```python
import math

import jax
import jax.numpy as jnp
import numpy as np
from jax import lax
from jax.experimental import pallas as pl
from jax.experimental.pallas import tpu as pltpu
from jax.sharding import Mesh, PartitionSpec as P

NT = 2048
NF = 64
F_LOW = 96
K = 1024

AXES = ("yh", "z1", "z0", "x", "yl", "core")
AF = ("yh", "z1", "z0", "x")
ROW = ("yl", "core")
GROUP = ("yh", "z0", "x", "yl", "core")
HOPS = (2, 1, 3)
SLOTS = (0,) + HOPS

VMEM = pl.BlockSpec(memory_space=pltpu.VMEM)
SMEM = pl.BlockSpec(memory_space=pltpu.SMEM)
HBM = pl.BlockSpec(memory_space=pl.ANY)


def tables(amplitude):
    samples = np.arange(NT, dtype=np.int64)
    frequency = F_LOW + np.arange(NF, dtype=np.int64)
    phase_index = frequency[:, None] * samples[None, :] % NT
    angles = phase_index.astype(np.float64) * (2.0 * math.pi / NT)
    both = np.stack([np.cos(angles), -np.sin(angles)], axis=1) * amplitude
    return both.astype(jnp.bfloat16)


def mover(sizes, order):
    n = math.prod(sizes)
    source = np.arange(n).reshape(sizes).transpose(order).reshape(-1)
    matrix = np.zeros((n, n), np.float32)
    matrix[source, np.arange(n)] = 1.0
    return matrix.astype(jnp.bfloat16)


def dot(a, b, dims=((1,), (0,))):
    return lax.dot_general(a, b, (dims, ((), ())), preferred_element_type=jnp.float32)


def receiver_kernel(x_hbm, table_hbm, mover_hbm, out_ref, x, table, moves, arrived, rows):
    copies = [
        pltpu.make_async_copy(table_hbm, table, arrived.at[0]),
        pltpu.make_async_copy(x_hbm, x, arrived.at[1]),
        pltpu.make_async_copy(mover_hbm, moves, arrived.at[2]),
    ]
    for copy in copies:
        copy.start()
    copies[0].wait()
    copies[1].wait()
    spectra = dot(x[...].reshape(512, NT), table[...]).astype(jnp.bfloat16)
    copies[2].wait()
    moved = dot(spectra, moves[...], ((0,), (0,)))
    low = lax.broadcasted_iota(jnp.int32, (NF, 128), 1) < 64
    for pair in range(4):
        real = moved[:NF, pair * 128 : (pair + 1) * 128]
        imag = moved[NF:, pair * 128 : (pair + 1) * 128]
        even = jnp.where(low, real, pltpu.roll(imag, 64, 1))
        odd = jnp.where(low, pltpu.roll(real, 64, 1), imag)
        rows[pl.ds(2 * pair, NF, stride=8), :] = even
        rows[pl.ds(2 * pair + 1, NF, stride=8), :] = odd
    out_ref[...] = rows[...].astype(jnp.bfloat16)


def receiver_spectra(traces, table):
    return pl.pallas_call(
        receiver_kernel,
        out_shape=jax.ShapeDtypeStruct((NF * 8, 128), jnp.bfloat16),
        in_specs=[HBM] * 3,
        out_specs=VMEM,
        scratch_shapes=[
            pltpu.VMEM((32, 16, NT), jnp.bfloat16),
            pltpu.VMEM((NT, 128), jnp.bfloat16),
            pltpu.VMEM((512, 512), jnp.bfloat16),
            pltpu.SemaphoreType.DMA((3,)),
            pltpu.VMEM((NF * 8, 128), jnp.float32),
        ],
        compiler_params=pltpu.CompilerParams(vmem_limit_bytes=60 << 20),
        cost_estimate=pl.CostEstimate(
            flops=2 * 512 * 128 * NT, bytes_accessed=3 << 20, transcendentals=0
        ),
        name="receiver_spectra",
    )(traces, table, jnp.asarray(mover((32, 8, 2), (1, 2, 0))))


AT_ONCE = 2


def source_kernel(x_hbm, own_hbm, table_hbm, out_ref, x, own, table, arrived, ready, rows):
    others = [
        pltpu.make_async_copy(table_hbm, table, ready.at[0]),
        pltpu.make_async_copy(own_hbm, own, ready.at[1]),
    ]
    others[0].start()
    for s in range(8):
        pltpu.make_async_copy(x_hbm.at[s], x.at[s], arrived.at[s]).start()
    others[1].start()
    others[0].wait()

    @pl.loop(0, 8 // AT_ONCE)
    def _(step):
        first = step * AT_ONCE
        for j in range(AT_ONCE):
            s = first + j
            pltpu.make_async_copy(x_hbm.at[s], x.at[s], arrived.at[s]).wait()
        traces = x[pl.ds(first, AT_ONCE)].reshape(AT_ONCE * 256, NT)
        spectra = dot(traces, table[...]).T
        for j in range(AT_ONCE):
            for c in range(2):
                for kh in range(2):
                    at = j * 256 + kh * 128
                    rows[pl.ds(kh * 16 + c * 8 + first + j, NF, stride=32), :] = spectra[
                        c * NF : (c + 1) * NF, at : at + 128
                    ]

    others[1].wait()
    out_ref[:, :32, :] = rows[...].astype(jnp.bfloat16).reshape(NF, 32, 128)
    out_ref[:, 32:40, :] = own[...].reshape(NF, 8, 128)


def source_spectra(traces, own, table):
    return pl.pallas_call(
        source_kernel,
        out_shape=jax.ShapeDtypeStruct((NF, 64, 128), jnp.bfloat16),
        in_specs=[HBM] * 3,
        out_specs=VMEM,
        scratch_shapes=[
            pltpu.VMEM((8, 256, NT), jnp.bfloat16),
            pltpu.VMEM((NF * 8, 128), jnp.bfloat16),
            pltpu.VMEM((NT, 128), jnp.bfloat16),
            pltpu.SemaphoreType.DMA((8,)),
            pltpu.SemaphoreType.DMA((2,)),
            pltpu.VMEM((NF * 32, 128), jnp.float32),
        ],
        compiler_params=pltpu.CompilerParams(vmem_limit_bytes=60 << 20),
        cost_estimate=pl.CostEstimate(
            flops=2 * 2048 * 128 * NT, bytes_accessed=10 << 20, transcendentals=0
        ),
        name="source_spectra",
    )(traces, own, table)


def product_kernel(z1_ref, wave_ref, got_ref, mover_ref, back_ref, out_ref, right, pred, rows):
    z1 = z1_ref[0]
    raw = jnp.zeros((256, 256), jnp.float32)
    for pair in range(2):
        at = 32 + 16 * pair
        pieces = [got_ref[:, row, at : at + 16, :].reshape(256, 128) for row in range(4)]
        moved = dot(jnp.concatenate(pieces, axis=1), mover_ref[...]).reshape(2, 8, 2, 8, 512)
        for half in range(2):
            slot = 2 * pair + half
            origin = lax.rem(z1 - SLOTS[slot] + 4, 4)
            left = []
            for yh in range(2):
                panel = 2 * yh + lax.div(origin, 2)
                start = pl.multiple_of(16 * lax.rem(origin, 2), 16)
                left.append(got_ref[:, panel, pl.ds(start, 16), :].reshape(256, 128))
                part = moved[yh, :, half].reshape(64, 512)
                for k in range(2):
                    for c in range(2):
                        at = 256 * k + 128 * c
                        right[slot, c, pl.ds(yh * 128 + k, 64, stride=2), :] = part[:, at : at + 128]
            coupled = jnp.concatenate([right[slot, 0], right[slot, 1]], axis=1)
            raw += dot(
                jnp.concatenate(left, axis=1),
                coupled.astype(jnp.bfloat16),
            )
    raw = raw.reshape(16, 2, 8, 256)
    real = raw[:, 0, :, :128] - raw[:, 1, :, 128:]
    imag = raw[:, 0, :, 128:] + raw[:, 1, :, :128]
    amplitude = 1.0 / math.sqrt(K)
    wave_real, wave_imag = wave_ref[0], wave_ref[1]
    pred[0] = ((real * wave_real - imag * wave_imag) * amplitude).reshape(128, 128)
    pred[1] = ((real * wave_imag + imag * wave_real) * amplitude).reshape(128, 128)
    wide = []
    for c in range(2):
        for high in range(2):
            wide.append(
                jnp.concatenate(
                    [pred[c, pl.ds(high * 4 + low, 16, stride=8), :] for low in range(4)], axis=1
                )
            )
    wide = dot(jnp.concatenate(wide, axis=0).astype(jnp.bfloat16), back_ref[...])
    for q in range(4):
        for row in range(4):
            rows[pl.ds(row * 4 + q, 16, stride=16), :] = wide[
                q * 16 : (q + 1) * 16, row * 128 : (row + 1) * 128
            ]
    out_ref[...] = rows[...].astype(jnp.bfloat16)


def predicted_spectra(got, z1, wavelet):
    return pl.pallas_call(
        product_kernel,
        out_shape=jax.ShapeDtypeStruct((256, 128), jnp.bfloat16),
        in_specs=[SMEM, SMEM] + [VMEM] * 3,
        out_specs=VMEM,
        scratch_shapes=[
            pltpu.VMEM((4, 2, 256, 128), jnp.float32),
            pltpu.VMEM((2, 128, 128), jnp.float32),
            pltpu.VMEM((256, 128), jnp.float32),
        ],
        compiler_params=pltpu.CompilerParams(vmem_limit_bytes=16 << 20),
        cost_estimate=pl.CostEstimate(flops=4 << 28, bytes_accessed=2 << 20, transcendentals=0),
        name="predicted_spectra",
    )(
        z1,
        wavelet,
        got.reshape(16, 4, 64, 128),
        jnp.asarray(mover((4, 2, 2, 32), (2, 1, 0, 3))),
        jnp.asarray(mover((4, 4, 32), (1, 0, 2))),
    )


def multiples_kernel(x_ref, table_ref, out_ref, rows):
    rows[...] = x_ref[...].astype(jnp.float32)
    half = rows[pl.ds(pl.program_id(0), 128, stride=2), :].astype(jnp.bfloat16)
    out_ref[...] = dot(half, table_ref[...], ((0,), (0,))).astype(jnp.bfloat16)


def multiples(returned):
    table = jnp.asarray(tables(1.0 / math.sqrt(NF)).reshape(2 * NF, NT))
    return pl.pallas_call(
        multiples_kernel,
        grid=(2,),
        out_shape=jax.ShapeDtypeStruct((256, NT), jnp.bfloat16),
        in_specs=[
            pl.BlockSpec((256, 128), lambda i: (0, 0)),
            pl.BlockSpec((128, NT), lambda i: (0, 0)),
        ],
        out_specs=pl.BlockSpec((128, NT), lambda i: (i, 0)),
        scratch_shapes=[pltpu.VMEM((256, 128), jnp.float32)],
        compiler_params=pltpu.CompilerParams(vmem_limit_bytes=24 << 20),
        cost_estimate=pl.CostEstimate(
            flops=2 * 256 * 128 * NT, bytes_accessed=2 << 20, transcendentals=0
        ),
        name="multiples",
    )(returned, table)


def per_device(source_traces, receiver_traces, wavelet_inverse):
    table = jnp.asarray(tables(1.0 / math.sqrt(NT)).transpose(2, 1, 0).reshape(NT, 2 * NF))
    own = receiver_spectra(receiver_traces, table)
    others = [lax.ppermute(own, "z1", [(i, (i + hop) % 4) for i in range(4)]) for hop in HOPS]
    sent = source_spectra(source_traces, own, table)
    others = jnp.concatenate([other.reshape(NF, 8, 128) for other in others], axis=1)
    sent = lax.dynamic_update_slice(sent, others, (0, 40, 0))
    got = lax.all_to_all(sent, GROUP, split_axis=0, concat_axis=0, tiled=True)
    wavelet = lax.dynamic_slice_in_dim(wavelet_inverse, lax.axis_index(GROUP), 1, 0).reshape(2)
    predicted = predicted_spectra(got, lax.axis_index("z1").reshape(1), wavelet)
    returned = lax.all_to_all(
        predicted.reshape(NF, 4, 128), GROUP, split_axis=0, concat_axis=0, tiled=True
    )
    return multiples(returned.reshape(256, 128)).reshape(8, 32, NT)


def solution(mesh):
    fine = Mesh(np.asarray(mesh.devices).reshape(2, 4, 2, 4, 2, 2), AXES)
    return jax.shard_map(
        per_device,
        mesh=fine,
        in_specs=(P(AF, ROW, None), P(ROW, AF, None), P()),
        out_specs=P(AF, ROW, None),
        check_vma=False,
    )
```

```python
import math

import jax
import jax.numpy as jnp
import numpy as np
from jax import lax
from jax.experimental import pallas as pl
from jax.experimental.pallas import tpu as pltpu
from jax.sharding import Mesh, PartitionSpec as P

NT = 2048
NF = 64
F_LOW = 96
K = 1024

AXES = ("yh", "z1", "z0", "x", "yl", "core")
AF = ("yh", "z1", "z0", "x")
ROW = ("yl", "core")
GROUP = ("yh", "z0", "x", "yl", "core")
HOPS = (1, 3, 2)
SLOTS = (0,) + HOPS

VMEM = pl.BlockSpec(memory_space=pltpu.VMEM)
SMEM = pl.BlockSpec(memory_space=pltpu.SMEM)
HBM = pl.BlockSpec(memory_space=pl.ANY)


def tables(amplitude):
    samples = np.arange(NT, dtype=np.int64)
    frequency = F_LOW + np.arange(NF, dtype=np.int64)
    phase_index = frequency[:, None] * samples[None, :] % NT
    angles = phase_index.astype(np.float64) * (2.0 * math.pi / NT)
    both = np.stack([np.cos(angles), -np.sin(angles)], axis=1) * amplitude
    return both.astype(jnp.bfloat16)


def mover(sizes, order):
    n = math.prod(sizes)
    source = np.arange(n).reshape(sizes).transpose(order).reshape(-1)
    matrix = np.zeros((n, n), np.float32)
    matrix[source, np.arange(n)] = 1.0
    return matrix.astype(jnp.bfloat16)


def dot(a, b, dims=((1,), (0,))):
    return lax.dot_general(a, b, (dims, ((), ())), preferred_element_type=jnp.float32)


def in_hbm(x):
    return pltpu.with_memory_space_constraint(x, pltpu.HBM)


AHEAD = 4


def receiver_kernel(
    x_hbm, source_hbm, table_hbm, mover_hbm, out_ref, ahead_ref, x, table, moves, arrived, rows
):
    copies = [
        pltpu.make_async_copy(table_hbm, table, arrived.at[0]),
        pltpu.make_async_copy(x_hbm, x, arrived.at[1]),
        pltpu.make_async_copy(mover_hbm, moves, arrived.at[2]),
        pltpu.make_async_copy(source_hbm.at[pl.ds(0, AHEAD)], ahead_ref, arrived.at[3]),
    ]
    for copy in copies:
        copy.start()
    copies[0].wait()
    copies[1].wait()
    spectra = dot(x[...].reshape(512, NT), table[...]).astype(jnp.bfloat16)
    copies[2].wait()
    moved = dot(spectra, moves[...], ((0,), (0,)))
    low = lax.broadcasted_iota(jnp.int32, (NF, 128), 1) < 64
    for pair in range(4):
        real = moved[:NF, pair * 128 : (pair + 1) * 128]
        imag = moved[NF:, pair * 128 : (pair + 1) * 128]
        even = jnp.where(low, real, pltpu.roll(imag, 64, 1))
        odd = jnp.where(low, pltpu.roll(real, 64, 1), imag)
        rows[pl.ds(2 * pair, NF, stride=8), :] = even
        rows[pl.ds(2 * pair + 1, NF, stride=8), :] = odd
    out_ref[...] = rows[...].astype(jnp.bfloat16)
    copies[3].wait()


def receiver_spectra(traces, source_traces, table):
    moves = jnp.asarray(mover((32, 8, 2), (1, 2, 0)))
    return pl.pallas_call(
        receiver_kernel,
        out_shape=[
            pltpu.VMEM((NF * 8, 128), jnp.bfloat16),
            pltpu.VMEM((AHEAD, 256, NT), jnp.bfloat16),
        ],
        in_specs=[HBM] * 4,
        out_specs=[VMEM] * 2,
        scratch_shapes=[
            pltpu.VMEM((32, 16, NT), jnp.bfloat16),
            pltpu.VMEM((NT, 128), jnp.bfloat16),
            pltpu.VMEM((512, 512), jnp.bfloat16),
            pltpu.SemaphoreType.DMA((4,)),
            pltpu.VMEM((NF * 8, 128), jnp.float32),
        ],
        compiler_params=pltpu.CompilerParams(vmem_limit_bytes=16 << 20),
        cost_estimate=pl.CostEstimate(
            flops=2 * 512 * 128 * NT, bytes_accessed=3 << 20, transcendentals=0
        ),
        name="receiver_spectra",
    )(in_hbm(traces), in_hbm(source_traces), in_hbm(table), in_hbm(moves))


AT_ONCE = 2


def source_kernel(x_hbm, ahead_ref, own_ref, table_hbm, out_ref, x, table, arrived, ready, rows):
    fetch = pltpu.make_async_copy(table_hbm, table, ready)
    fetch.start()
    for s in range(8 - AHEAD):
        pltpu.make_async_copy(x_hbm.at[AHEAD + s], x.at[s], arrived.at[s]).start()
    out_ref[:, 32:40, :] = own_ref[...].reshape(NF, 8, 128)
    fetch.wait()

    def transform(traces, first):
        spectra = dot(traces.reshape(AT_ONCE * 256, NT), table[...]).T
        for j in range(AT_ONCE):
            for c in range(2):
                for kh in range(2):
                    at = j * 256 + kh * 128
                    rows[pl.ds(kh * 16 + c * 8 + first + j, NF, stride=32), :] = spectra[
                        c * NF : (c + 1) * NF, at : at + 128
                    ]

    @pl.loop(0, AHEAD // AT_ONCE)
    def _(step):
        first = step * AT_ONCE
        transform(ahead_ref[pl.ds(first, AT_ONCE)], first)

    @pl.loop(0, (8 - AHEAD) // AT_ONCE)
    def _(step):
        first = step * AT_ONCE
        for j in range(AT_ONCE):
            s = first + j
            pltpu.make_async_copy(x_hbm.at[AHEAD + s], x.at[s], arrived.at[s]).wait()
        transform(x[pl.ds(first, AT_ONCE)], AHEAD + first)

    out_ref[:, :32, :] = rows[...].astype(jnp.bfloat16).reshape(NF, 32, 128)


def source_spectra(traces, ahead, own, table):
    return pl.pallas_call(
        source_kernel,
        out_shape=pltpu.VMEM((NF, 64, 128), jnp.bfloat16),
        in_specs=[HBM, VMEM, VMEM, HBM],
        out_specs=VMEM,
        scratch_shapes=[
            pltpu.VMEM((8 - AHEAD, 256, NT), jnp.bfloat16),
            pltpu.VMEM((NT, 128), jnp.bfloat16),
            pltpu.SemaphoreType.DMA((8 - AHEAD,)),
            pltpu.SemaphoreType.DMA,
            pltpu.VMEM((NF * 32, 128), jnp.float32),
        ],
        compiler_params=pltpu.CompilerParams(vmem_limit_bytes=16 << 20),
        cost_estimate=pl.CostEstimate(
            flops=2 * 2048 * 128 * NT, bytes_accessed=10 << 20, transcendentals=0
        ),
        name="source_spectra",
    )(in_hbm(traces), ahead, own, in_hbm(table))


def product_kernel(z1_ref, wave_ref, got_ref, mover_ref, back_ref, out_ref, right, pred, rows):
    z1 = z1_ref[0]
    raw = jnp.zeros((256, 256), jnp.float32)
    for pair in range(2):
        at = 32 + 16 * pair
        pieces = [got_ref[:, row, at : at + 16, :].reshape(256, 128) for row in range(4)]
        moved = dot(jnp.concatenate(pieces, axis=1), mover_ref[...]).reshape(2, 8, 2, 8, 512)
        for half in range(2):
            slot = 2 * pair + half
            origin = lax.rem(z1 - SLOTS[slot] + 4, 4)
            left = []
            for yh in range(2):
                panel = 2 * yh + lax.div(origin, 2)
                start = pl.multiple_of(16 * lax.rem(origin, 2), 16)
                left.append(got_ref[:, panel, pl.ds(start, 16), :].reshape(256, 128))
                part = moved[yh, :, half]
                if SLOTS[slot] == 2:
                    part = jnp.concatenate([part[4:], part[:4]], axis=0)
                part = part.reshape(64, 512)
                for k in range(2):
                    for c in range(2):
                        at = 256 * k + 128 * c
                        right[slot, c, pl.ds(yh * 128 + k, 64, stride=2), :] = part[:, at : at + 128]
            coupled = jnp.concatenate([right[slot, 0], right[slot, 1]], axis=1)
            raw += dot(
                jnp.concatenate(left, axis=1),
                coupled.astype(jnp.bfloat16),
            )
    raw = raw.reshape(16, 2, 8, 256)
    real = raw[:, 0, :, :128] - raw[:, 1, :, 128:]
    imag = raw[:, 0, :, 128:] + raw[:, 1, :, :128]
    amplitude = 1.0 / math.sqrt(K)
    wave_real, wave_imag = wave_ref[0], wave_ref[1]
    pred[0] = ((real * wave_real - imag * wave_imag) * amplitude).reshape(128, 128)
    pred[1] = ((real * wave_imag + imag * wave_real) * amplitude).reshape(128, 128)
    wide = []
    for c in range(2):
        for high in range(2):
            wide.append(
                jnp.concatenate(
                    [pred[c, pl.ds(high * 4 + low, 16, stride=8), :] for low in range(4)], axis=1
                )
            )
    wide = dot(jnp.concatenate(wide, axis=0).astype(jnp.bfloat16), back_ref[...])
    for q in range(4):
        for row in range(4):
            rows[pl.ds(row * 4 + q, 16, stride=16), :] = wide[
                q * 16 : (q + 1) * 16, row * 128 : (row + 1) * 128
            ]
    out_ref[...] = rows[...].astype(jnp.bfloat16)


def predicted_spectra(got, z1, wavelet):
    return pl.pallas_call(
        product_kernel,
        out_shape=jax.ShapeDtypeStruct((256, 128), jnp.bfloat16),
        in_specs=[SMEM, SMEM] + [VMEM] * 3,
        out_specs=VMEM,
        scratch_shapes=[
            pltpu.VMEM((4, 2, 256, 128), jnp.float32),
            pltpu.VMEM((2, 128, 128), jnp.float32),
            pltpu.VMEM((256, 128), jnp.float32),
        ],
        compiler_params=pltpu.CompilerParams(vmem_limit_bytes=16 << 20),
        cost_estimate=pl.CostEstimate(flops=4 << 28, bytes_accessed=2 << 20, transcendentals=0),
        name="predicted_spectra",
    )(
        z1,
        wavelet,
        got.reshape(16, 4, 64, 128),
        jnp.asarray(mover((4, 2, 2, 32), (2, 1, 0, 3))),
        jnp.asarray(mover((4, 4, 32), (1, 0, 2))),
    )


def multiples_kernel(x_ref, table_ref, out_ref, rows):
    rows[...] = x_ref[...].astype(jnp.float32)
    half = rows[pl.ds(pl.program_id(0), 128, stride=2), :].astype(jnp.bfloat16)
    out_ref[...] = dot(half, table_ref[...], ((0,), (0,))).astype(jnp.bfloat16)


def multiples(returned):
    table = jnp.asarray(tables(1.0 / math.sqrt(NF)).reshape(2 * NF, NT))
    return pl.pallas_call(
        multiples_kernel,
        grid=(2,),
        out_shape=jax.ShapeDtypeStruct((256, NT), jnp.bfloat16),
        in_specs=[
            pl.BlockSpec((256, 128), lambda i: (0, 0)),
            pl.BlockSpec((128, NT), lambda i: (0, 0)),
        ],
        out_specs=pl.BlockSpec((128, NT), lambda i: (i, 0)),
        scratch_shapes=[pltpu.VMEM((256, 128), jnp.float32)],
        compiler_params=pltpu.CompilerParams(vmem_limit_bytes=24 << 20),
        cost_estimate=pl.CostEstimate(
            flops=2 * 256 * 128 * NT, bytes_accessed=2 << 20, transcendentals=0
        ),
        name="multiples",
    )(returned, table)


def moves(hop):
    return [
        (2 * z1 + z0, 2 * ((z1 + hop) % 4) + (1 - z0 if hop == 2 else z0))
        for z1 in range(4)
        for z0 in range(2)
    ]


def per_device(source_traces, receiver_traces, wavelet_inverse):
    table = jnp.asarray(tables(1.0 / math.sqrt(NT)).transpose(2, 1, 0).reshape(NT, 2 * NF))
    own, ahead = receiver_spectra(receiver_traces, source_traces, table)
    others = [lax.ppermute(own, ("z1", "z0"), moves(hop)) for hop in HOPS]
    sent = source_spectra(source_traces, ahead, own, table)
    others = jnp.concatenate([other.reshape(NF, 8, 128) for other in others], axis=1)
    sent = lax.dynamic_update_slice(sent, others, (0, 40, 0))
    got = lax.all_to_all(sent, GROUP, split_axis=0, concat_axis=0, tiled=True)
    wavelet = lax.dynamic_slice_in_dim(wavelet_inverse, lax.axis_index(GROUP), 1, 0).reshape(2)
    predicted = predicted_spectra(got, lax.axis_index("z1").reshape(1), wavelet)
    returned = lax.all_to_all(
        predicted.reshape(NF, 4, 128), GROUP, split_axis=0, concat_axis=0, tiled=True
    )
    return multiples(returned.reshape(256, 128)).reshape(8, 32, NT)


def solution(mesh):
    fine = Mesh(np.asarray(mesh.devices).reshape(2, 4, 2, 4, 2, 2), AXES)
    return jax.shard_map(
        per_device,
        mesh=fine,
        in_specs=(P(AF, ROW, None), P(ROW, AF, None), P()),
        out_specs=P(AF, ROW, None),
        check_vma=False,
    )
```

```python
import math

import jax
import jax.numpy as jnp
import numpy as np
from jax import lax
from jax.experimental import pallas as pl
from jax.experimental.pallas import tpu as pltpu
from jax.sharding import Mesh, PartitionSpec as P

NT = 2048
NF = 64
F_LOW = 96
K = 1024

AXES = ("yh", "z1", "z0", "x", "yl", "core")
AF = ("yh", "z1", "z0", "x")
ROW = ("yl", "core")
GROUP = ("yh", "z0", "x", "yl", "core")
HOPS = (3, 1, 2)
SLOTS = (0,) + HOPS

VMEM = pl.BlockSpec(memory_space=pltpu.VMEM)
SMEM = pl.BlockSpec(memory_space=pltpu.SMEM)
HBM = pl.BlockSpec(memory_space=pl.ANY)


def tables(amplitude):
    samples = np.arange(NT, dtype=np.int64)
    frequency = F_LOW + np.arange(NF, dtype=np.int64)
    phase_index = frequency[:, None] * samples[None, :] % NT
    angles = phase_index.astype(np.float64) * (2.0 * math.pi / NT)
    both = np.stack([np.cos(angles), -np.sin(angles)], axis=1) * amplitude
    return both.astype(jnp.bfloat16)


def mover(sizes, order):
    n = math.prod(sizes)
    source = np.arange(n).reshape(sizes).transpose(order).reshape(-1)
    matrix = np.zeros((n, n), np.float32)
    matrix[source, np.arange(n)] = 1.0
    return matrix.astype(jnp.bfloat16)


def dot(a, b, dims=((1,), (0,))):
    return lax.dot_general(a, b, (dims, ((), ())), preferred_element_type=jnp.float32)


def in_hbm(x):
    return pltpu.with_memory_space_constraint(x, pltpu.HBM)


def receiver_kernel(
    x_hbm, table_hbm, mover_hbm, out_ref, x, table, moves, arrived, rows
):
    copies = [
        pltpu.make_async_copy(table_hbm, table, arrived.at[0]),
        pltpu.make_async_copy(x_hbm, x, arrived.at[1]),
        pltpu.make_async_copy(mover_hbm, moves, arrived.at[2]),
    ]
    for copy in copies:
        copy.start()
    copies[0].wait()
    copies[1].wait()
    spectra = dot(x[...].reshape(512, NT), table[...]).astype(jnp.bfloat16)
    copies[2].wait()
    moved = dot(spectra, moves[...], ((0,), (0,)))
    low = lax.broadcasted_iota(jnp.int32, (NF, 128), 1) < 64
    for pair in range(4):
        real = moved[:NF, pair * 128 : (pair + 1) * 128]
        imag = moved[NF:, pair * 128 : (pair + 1) * 128]
        even = jnp.where(low, real, pltpu.roll(imag, 64, 1))
        odd = jnp.where(low, pltpu.roll(real, 64, 1), imag)
        rows[pl.ds(2 * pair, NF, stride=8), :] = even
        rows[pl.ds(2 * pair + 1, NF, stride=8), :] = odd
    out_ref[...] = rows[...].astype(jnp.bfloat16)


def receiver_spectra(traces, table):
    moves = jnp.asarray(mover((32, 8, 2), (1, 2, 0)))
    return pl.pallas_call(
        receiver_kernel,
        out_shape=pltpu.VMEM((NF * 8, 128), jnp.bfloat16),
        in_specs=[HBM] * 3,
        out_specs=VMEM,
        scratch_shapes=[
            pltpu.VMEM((32, 16, NT), jnp.bfloat16),
            pltpu.VMEM((NT, 128), jnp.bfloat16),
            pltpu.VMEM((512, 512), jnp.bfloat16),
            pltpu.SemaphoreType.DMA((3,)),
            pltpu.VMEM((NF * 8, 128), jnp.float32),
        ],
        compiler_params=pltpu.CompilerParams(vmem_limit_bytes=16 << 20),
        cost_estimate=pl.CostEstimate(
            flops=200 * 512 * 128 * NT, bytes_accessed=3 << 20, transcendentals=0
        ),
        name="receiver_spectra",
    )(in_hbm(traces), in_hbm(table), in_hbm(moves))


AT_ONCE = 2


def source_kernel(x_ref, own_ref, table_ref, out_ref, rows):
    out_ref[:, 32:40, :] = own_ref[...].reshape(NF, 8, 128)

    @pl.loop(0, 8 // AT_ONCE)
    def _(step):
        first = step * AT_ONCE
        traces = x_ref[pl.ds(first, AT_ONCE)].reshape(AT_ONCE * 256, NT)
        spectra = dot(traces, table_ref[...]).T
        for j in range(AT_ONCE):
            for c in range(2):
                for kh in range(2):
                    at = j * 256 + kh * 128
                    rows[pl.ds(kh * 16 + c * 8 + first + j, NF, stride=32), :] = spectra[
                        c * NF : (c + 1) * NF, at : at + 128
                    ]

    out_ref[:, :32, :] = rows[...].astype(jnp.bfloat16).reshape(NF, 32, 128)


def source_spectra(traces, own, table):
    return pl.pallas_call(
        source_kernel,
        out_shape=jax.ShapeDtypeStruct((NF, 64, 128), jnp.bfloat16),
        in_specs=[VMEM] * 3,
        out_specs=VMEM,
        scratch_shapes=[pltpu.VMEM((NF * 32, 128), jnp.float32)],
        compiler_params=pltpu.CompilerParams(vmem_limit_bytes=8 << 20),
        cost_estimate=pl.CostEstimate(
            flops=2 * 2048 * 128 * NT, bytes_accessed=10 << 20, transcendentals=0
        ),
        name="source_spectra",
    )(traces, own, table)


def product_kernel(z1_ref, wave_ref, got_ref, mover_ref, back_ref, out_ref, right, pred, rows):
    z1 = z1_ref[0]
    raw = jnp.zeros((256, 256), jnp.float32)
    for pair in range(2):
        at = 32 + 16 * pair
        pieces = [got_ref[:, row, at : at + 16, :].reshape(256, 128) for row in range(4)]
        moved = dot(jnp.concatenate(pieces, axis=1), mover_ref[...]).reshape(2, 8, 2, 8, 512)
        for half in range(2):
            slot = 2 * pair + half
            origin = lax.rem(z1 - SLOTS[slot] + 4, 4)
            left = []
            for yh in range(2):
                panel = 2 * yh + lax.div(origin, 2)
                start = pl.multiple_of(16 * lax.rem(origin, 2), 16)
                left.append(got_ref[:, panel, pl.ds(start, 16), :].reshape(256, 128))
                part = moved[yh, :, half]
                if SLOTS[slot] == 2:
                    part = jnp.concatenate([part[4:], part[:4]], axis=0)
                part = part.reshape(64, 512)
                for k in range(2):
                    for c in range(2):
                        at = 256 * k + 128 * c
                        right[slot, c, pl.ds(yh * 128 + k, 64, stride=2), :] = part[:, at : at + 128]
            coupled = jnp.concatenate([right[slot, 0], right[slot, 1]], axis=1)
            raw += dot(
                jnp.concatenate(left, axis=1),
                coupled.astype(jnp.bfloat16),
            )
    raw = raw.reshape(16, 2, 8, 256)
    real = raw[:, 0, :, :128] - raw[:, 1, :, 128:]
    imag = raw[:, 0, :, 128:] + raw[:, 1, :, :128]
    amplitude = 1.0 / math.sqrt(K)
    wave_real, wave_imag = wave_ref[0], wave_ref[1]
    pred[0] = ((real * wave_real - imag * wave_imag) * amplitude).reshape(128, 128)
    pred[1] = ((real * wave_imag + imag * wave_real) * amplitude).reshape(128, 128)
    wide = []
    for c in range(2):
        for high in range(2):
            wide.append(
                jnp.concatenate(
                    [pred[c, pl.ds(high * 4 + low, 16, stride=8), :] for low in range(4)], axis=1
                )
            )
    wide = dot(jnp.concatenate(wide, axis=0).astype(jnp.bfloat16), back_ref[...])
    for q in range(4):
        for row in range(4):
            rows[pl.ds(row * 4 + q, 16, stride=16), :] = wide[
                q * 16 : (q + 1) * 16, row * 128 : (row + 1) * 128
            ]
    out_ref[...] = rows[...].astype(jnp.bfloat16)


def predicted_spectra(got, z1, wavelet):
    return pl.pallas_call(
        product_kernel,
        out_shape=jax.ShapeDtypeStruct((256, 128), jnp.bfloat16),
        in_specs=[SMEM, SMEM] + [VMEM] * 3,
        out_specs=VMEM,
        scratch_shapes=[
            pltpu.VMEM((4, 2, 256, 128), jnp.float32),
            pltpu.VMEM((2, 128, 128), jnp.float32),
            pltpu.VMEM((256, 128), jnp.float32),
        ],
        compiler_params=pltpu.CompilerParams(vmem_limit_bytes=16 << 20),
        cost_estimate=pl.CostEstimate(flops=4 << 28, bytes_accessed=2 << 20, transcendentals=0),
        name="predicted_spectra",
    )(
        z1,
        wavelet,
        got.reshape(16, 4, 64, 128),
        jnp.asarray(mover((4, 2, 2, 32), (2, 1, 0, 3))),
        jnp.asarray(mover((4, 4, 32), (1, 0, 2))),
    )


def multiples_kernel(x_ref, table_ref, out_hbm, rows, stage, sent):
    rows[...] = x_ref[...].astype(jnp.float32)
    copies = []
    for high in range(2):
        half = rows[pl.ds(high, 128, stride=2), :].astype(jnp.bfloat16).T
        for part in range(2):
            at = 1024 * part
            stage[128 * high : 128 * high + 128, at : at + 1024] = dot(
                half, table_ref[:, at : at + 1024]
            ).astype(jnp.bfloat16)
            here = (pl.ds(128 * high, 128), pl.ds(at, 1024))
            copy = pltpu.make_async_copy(stage.at[here], out_hbm.at[here], sent.at[len(copies)])
            copy.start()
            copies.append(copy)
    for copy in copies:
        copy.wait()


def multiples(returned):
    table = jnp.asarray(tables(1.0 / math.sqrt(NF)).reshape(2 * NF, NT))
    return pl.pallas_call(
        multiples_kernel,
        out_shape=jax.ShapeDtypeStruct((256, NT), jnp.bfloat16),
        in_specs=[VMEM, VMEM],
        out_specs=HBM,
        scratch_shapes=[
            pltpu.VMEM((256, 128), jnp.float32),
            pltpu.VMEM((256, NT), jnp.bfloat16),
            pltpu.SemaphoreType.DMA((4,)),
        ],
        compiler_params=pltpu.CompilerParams(vmem_limit_bytes=16 << 20),
        cost_estimate=pl.CostEstimate(
            flops=2 * 256 * 128 * NT, bytes_accessed=2 << 20, transcendentals=0
        ),
        name="multiples",
    )(returned, table)


def moves(hop):
    return [
        (2 * z1 + z0, 2 * ((z1 + hop) % 4) + (1 - z0 if hop == 2 else z0))
        for z1 in range(4)
        for z0 in range(2)
    ]


def per_device(source_traces, receiver_traces, wavelet_inverse):
    table = jnp.asarray(tables(1.0 / math.sqrt(NT)).transpose(2, 1, 0).reshape(NT, 2 * NF))
    own = receiver_spectra(receiver_traces, table)
    others = [lax.ppermute(own, ("z1", "z0"), moves(hop)) for hop in HOPS]
    sent = source_spectra(source_traces, own, table)
    others = jnp.concatenate([other.reshape(NF, 8, 128) for other in others], axis=1)
    sent = lax.dynamic_update_slice(sent, others, (0, 40, 0))
    got = lax.all_to_all(sent, GROUP, split_axis=0, concat_axis=0, tiled=True)
    wavelet = lax.dynamic_slice_in_dim(wavelet_inverse, lax.axis_index(GROUP), 1, 0).reshape(2)
    predicted = predicted_spectra(got, lax.axis_index("z1").reshape(1), wavelet)
    returned = lax.all_to_all(
        predicted.reshape(NF, 4, 128), GROUP, split_axis=0, concat_axis=0, tiled=True
    )
    return multiples(returned.reshape(256, 128)).reshape(8, 32, NT)


def solution(mesh):
    fine = Mesh(np.asarray(mesh.devices).reshape(2, 4, 2, 4, 2, 2), AXES)
    return jax.shard_map(
        per_device,
        mesh=fine,
        in_specs=(P(AF, ROW, None), P(ROW, AF, None), P()),
        out_specs=P(AF, ROW, None),
        check_vma=False,
    )
```

```python
import math

import jax
import jax.numpy as jnp
import numpy as np
from jax import lax
from jax.experimental import pallas as pl
from jax.experimental.pallas import tpu as pltpu
from jax.sharding import Mesh, PartitionSpec as P

NT = 2048
NF = 64
F_LOW = 96
K = 1024

AXES = ("yh", "z1", "z0", "x", "yl", "core")
AF = ("yh", "z1", "z0", "x")
ROW = ("yl", "core")
GROUP = ("yh", "z0", "x", "yl", "core")
HOPS = (3, 1, 2)
SLOTS = (0,) + HOPS

VMEM = pl.BlockSpec(memory_space=pltpu.VMEM)
SMEM = pl.BlockSpec(memory_space=pltpu.SMEM)
HBM = pl.BlockSpec(memory_space=pl.ANY)


def tables(amplitude):
    samples = np.arange(NT, dtype=np.int64)
    frequency = F_LOW + np.arange(NF, dtype=np.int64)
    phase_index = frequency[:, None] * samples[None, :] % NT
    angles = phase_index.astype(np.float64) * (2.0 * math.pi / NT)
    both = np.stack([np.cos(angles), -np.sin(angles)], axis=1) * amplitude
    return both.astype(jnp.bfloat16)


def mover(sizes, order):
    n = math.prod(sizes)
    source = np.arange(n).reshape(sizes).transpose(order).reshape(-1)
    matrix = np.zeros((n, n), np.float32)
    matrix[source, np.arange(n)] = 1.0
    return matrix.astype(jnp.bfloat16)


def dot(a, b, dims=((1,), (0,))):
    return lax.dot_general(a, b, (dims, ((), ())), preferred_element_type=jnp.float32)


def in_hbm(x):
    return pltpu.with_memory_space_constraint(x, pltpu.HBM)


def receiver_kernel(
    x_hbm, table_hbm, mover_hbm, out_ref, x, table, moves, arrived, rows
):
    copies = [
        pltpu.make_async_copy(table_hbm, table, arrived.at[0]),
        pltpu.make_async_copy(x_hbm, x, arrived.at[1]),
        pltpu.make_async_copy(mover_hbm, moves, arrived.at[2]),
    ]
    for copy in copies:
        copy.start()
    copies[0].wait()
    copies[1].wait()
    spectra = dot(x[...].reshape(512, NT), table[...]).astype(jnp.bfloat16)
    copies[2].wait()
    moved = dot(spectra, moves[...], ((0,), (0,)))
    low = lax.broadcasted_iota(jnp.int32, (NF, 128), 1) < 64
    for pair in range(4):
        real = moved[:NF, pair * 128 : (pair + 1) * 128]
        imag = moved[NF:, pair * 128 : (pair + 1) * 128]
        even = jnp.where(low, real, pltpu.roll(imag, 64, 1))
        odd = jnp.where(low, pltpu.roll(real, 64, 1), imag)
        rows[pl.ds(2 * pair, NF, stride=8), :] = even
        rows[pl.ds(2 * pair + 1, NF, stride=8), :] = odd
    out_ref[...] = rows[...].astype(jnp.bfloat16)


def receiver_spectra(traces, table):
    moves = jnp.asarray(mover((32, 8, 2), (1, 2, 0)))
    return pl.pallas_call(
        receiver_kernel,
        out_shape=pltpu.VMEM((NF * 8, 128), jnp.bfloat16),
        in_specs=[HBM] * 3,
        out_specs=VMEM,
        scratch_shapes=[
            pltpu.VMEM((32, 16, NT), jnp.bfloat16),
            pltpu.VMEM((NT, 128), jnp.bfloat16),
            pltpu.VMEM((512, 512), jnp.bfloat16),
            pltpu.SemaphoreType.DMA((3,)),
            pltpu.VMEM((NF * 8, 128), jnp.float32),
        ],
        compiler_params=pltpu.CompilerParams(vmem_limit_bytes=16 << 20),
        cost_estimate=pl.CostEstimate(
            flops=200 * 512 * 128 * NT, bytes_accessed=3 << 20, transcendentals=0
        ),
        name="receiver_spectra",
    )(in_hbm(traces), in_hbm(table), in_hbm(moves))


AT_ONCE = 2


def source_kernel(x_ref, own_ref, table_ref, out_ref, rows):
    out_ref[:, 32:40, :] = own_ref[...].reshape(NF, 8, 128)

    @pl.loop(0, 8 // AT_ONCE)
    def _(step):
        first = step * AT_ONCE
        traces = x_ref[pl.ds(first, AT_ONCE)].reshape(AT_ONCE * 256, NT)
        spectra = dot(traces, table_ref[...]).T
        for j in range(AT_ONCE):
            for c in range(2):
                for kh in range(2):
                    at = j * 256 + kh * 128
                    rows[pl.ds(kh * 16 + c * 8 + first + j, NF, stride=32), :] = spectra[
                        c * NF : (c + 1) * NF, at : at + 128
                    ]

    out_ref[:, :32, :] = rows[...].astype(jnp.bfloat16).reshape(NF, 32, 128)


def source_spectra(traces, own, table):
    return pl.pallas_call(
        source_kernel,
        out_shape=jax.ShapeDtypeStruct((NF, 64, 128), jnp.bfloat16),
        in_specs=[VMEM] * 3,
        out_specs=VMEM,
        scratch_shapes=[pltpu.VMEM((NF * 32, 128), jnp.float32)],
        compiler_params=pltpu.CompilerParams(vmem_limit_bytes=8 << 20),
        cost_estimate=pl.CostEstimate(
            flops=2 * 2048 * 128 * NT, bytes_accessed=10 << 20, transcendentals=0
        ),
        name="source_spectra",
    )(traces, own, table)


def swapped(tiles):
    group = lax.broadcasted_iota(jnp.int32, tiles[0].shape, 1) // 32
    for bit in (1, 2):
        keep = (group & bit) == 0
        tiles = list(tiles)
        for i in range(4):
            if not i & bit:
                a, b = tiles[i], tiles[i + bit]
                tiles[i] = jnp.where(keep, a, pltpu.roll(b, 32 * bit, 1))
                tiles[i + bit] = jnp.where(keep, pltpu.roll(a, 128 - 32 * bit, 1), b)
    return tiles


def product_kernel(z1_ref, wave_ref, got_ref, out_ref, right, pred, rows):
    z1 = z1_ref[0]
    raw = jnp.zeros((256, 256), jnp.float32)
    for pair in range(2):
        at = 32 + 16 * pair
        pieces = [
            got_ref[:, row, at : at + 16, :].reshape(256, 128).astype(jnp.float32) for row in range(4)
        ]
        tiles = [tile.reshape(2, 8, 2, 8, 128) for tile in swapped(pieces)]
        for half in range(2):
            slot = 2 * pair + half
            origin = lax.rem(z1 - SLOTS[slot] + 4, 4)
            left = []
            for yh in range(2):
                panel = 2 * yh + lax.div(origin, 2)
                start = pl.multiple_of(16 * lax.rem(origin, 2), 16)
                left.append(got_ref[:, panel, pl.ds(start, 16), :].reshape(256, 128))
                for k in range(2):
                    for c in range(2):
                        part = tiles[2 * c + k][yh, :, half]
                        if SLOTS[slot] == 2:
                            part = jnp.concatenate([part[4:], part[:4]], axis=0)
                        right[slot, c, pl.ds(yh * 128 + k, 64, stride=2), :] = part.reshape(64, 128)
            coupled = jnp.concatenate([right[slot, 0], right[slot, 1]], axis=1)
            raw += dot(
                jnp.concatenate(left, axis=1),
                coupled.astype(jnp.bfloat16),
            )
    raw = raw.reshape(16, 2, 8, 256)
    real = raw[:, 0, :, :128] - raw[:, 1, :, 128:]
    imag = raw[:, 0, :, 128:] + raw[:, 1, :, :128]
    amplitude = 1.0 / math.sqrt(K)
    wave_real, wave_imag = wave_ref[0], wave_ref[1]
    pred[0] = ((real * wave_real - imag * wave_imag) * amplitude).reshape(128, 128)
    pred[1] = ((real * wave_imag + imag * wave_real) * amplitude).reshape(128, 128)
    wide = [
        jnp.concatenate(
            [
                pred[c, pl.ds(high * 4 + low, 16, stride=8), :]
                for c in range(2)
                for high in range(2)
            ],
            axis=0,
        )
        for low in range(4)
    ]
    for row, tile in enumerate(swapped(wide)):
        for q in range(4):
            rows[pl.ds(row * 4 + q, 16, stride=16), :] = tile[q * 16 : (q + 1) * 16]
    out_ref[...] = rows[...].astype(jnp.bfloat16)


def predicted_spectra(got, z1, wavelet):
    return pl.pallas_call(
        product_kernel,
        out_shape=jax.ShapeDtypeStruct((256, 128), jnp.bfloat16),
        in_specs=[SMEM, SMEM, VMEM],
        out_specs=VMEM,
        scratch_shapes=[
            pltpu.VMEM((4, 2, 256, 128), jnp.float32),
            pltpu.VMEM((2, 128, 128), jnp.float32),
            pltpu.VMEM((256, 128), jnp.float32),
        ],
        compiler_params=pltpu.CompilerParams(vmem_limit_bytes=16 << 20),
        cost_estimate=pl.CostEstimate(flops=4 << 28, bytes_accessed=2 << 20, transcendentals=0),
        name="predicted_spectra",
    )(
        z1,
        wavelet,
        got.reshape(16, 4, 64, 128),
    )


def multiples_kernel(x_ref, table_ref, out_hbm, rows, stage, sent):
    rows[...] = x_ref[...].astype(jnp.float32)
    copies = []
    for high in range(2):
        half = rows[pl.ds(high, 128, stride=2), :].astype(jnp.bfloat16).T
        for part in range(2):
            at = 1024 * part
            stage[128 * high : 128 * high + 128, at : at + 1024] = dot(
                half, table_ref[:, at : at + 1024]
            ).astype(jnp.bfloat16)
            here = (pl.ds(128 * high, 128), pl.ds(at, 1024))
            copy = pltpu.make_async_copy(stage.at[here], out_hbm.at[here], sent.at[len(copies)])
            copy.start()
            copies.append(copy)
    for copy in copies:
        copy.wait()


def multiples(returned):
    table = jnp.asarray(tables(1.0 / math.sqrt(NF)).reshape(2 * NF, NT))
    return pl.pallas_call(
        multiples_kernel,
        out_shape=jax.ShapeDtypeStruct((256, NT), jnp.bfloat16),
        in_specs=[VMEM, VMEM],
        out_specs=HBM,
        scratch_shapes=[
            pltpu.VMEM((256, 128), jnp.float32),
            pltpu.VMEM((256, NT), jnp.bfloat16),
            pltpu.SemaphoreType.DMA((4,)),
        ],
        compiler_params=pltpu.CompilerParams(vmem_limit_bytes=16 << 20),
        cost_estimate=pl.CostEstimate(
            flops=2 * 256 * 128 * NT, bytes_accessed=2 << 20, transcendentals=0
        ),
        name="multiples",
    )(returned, table)


def moves(hop):
    return [
        (2 * z1 + z0, 2 * ((z1 + hop) % 4) + (1 - z0 if hop == 2 else z0))
        for z1 in range(4)
        for z0 in range(2)
    ]


def per_device(source_traces, receiver_traces, wavelet_inverse):
    table = jnp.asarray(tables(1.0 / math.sqrt(NT)).transpose(2, 1, 0).reshape(NT, 2 * NF))
    own = receiver_spectra(receiver_traces, table)
    others = [lax.ppermute(own, ("z1", "z0"), moves(hop)) for hop in HOPS]
    sent = source_spectra(source_traces, own, table)
    others = jnp.concatenate([other.reshape(NF, 8, 128) for other in others], axis=1)
    sent = lax.dynamic_update_slice(sent, others, (0, 40, 0))
    got = lax.all_to_all(sent, GROUP, split_axis=0, concat_axis=0, tiled=True)
    wavelet = lax.dynamic_slice_in_dim(wavelet_inverse, lax.axis_index(GROUP), 1, 0).reshape(2)
    predicted = predicted_spectra(got, lax.axis_index("z1").reshape(1), wavelet)
    returned = lax.all_to_all(
        predicted.reshape(NF, 4, 128), GROUP, split_axis=0, concat_axis=0, tiled=True
    )
    return multiples(returned.reshape(256, 128)).reshape(8, 32, NT)


def solution(mesh):
    fine = Mesh(np.asarray(mesh.devices).reshape(2, 4, 2, 4, 2, 2), AXES)
    return jax.shard_map(
        per_device,
        mesh=fine,
        in_specs=(P(AF, ROW, None), P(ROW, AF, None), P()),
        out_specs=P(AF, ROW, None),
        check_vma=False,
    )
```

```python
import math

import jax
import jax.numpy as jnp
import numpy as np
from jax import lax
from jax.experimental import pallas as pl
from jax.experimental.pallas import tpu as pltpu
from jax.sharding import Mesh, PartitionSpec as P

NT = 2048
NF = 64
F_LOW = 96
K = 1024

AXES = ("yh", "z1", "z0", "x", "yl", "core")
AF = ("yh", "z1", "z0", "x")
ROW = ("yl", "core")
GROUP = ("yh", "z0", "x", "yl", "core")
HOPS = (3, 1, 2)
SLOTS = (0,) + HOPS

VMEM = pl.BlockSpec(memory_space=pltpu.VMEM)
SMEM = pl.BlockSpec(memory_space=pltpu.SMEM)
HBM = pl.BlockSpec(memory_space=pl.ANY)


def tables(amplitude):
    samples = np.arange(NT, dtype=np.int64)
    frequency = F_LOW + np.arange(NF, dtype=np.int64)
    phase_index = frequency[:, None] * samples[None, :] % NT
    angles = phase_index.astype(np.float64) * (2.0 * math.pi / NT)
    both = np.stack([np.cos(angles), -np.sin(angles)], axis=1) * amplitude
    return both.astype(jnp.bfloat16)


def mover(sizes, order):
    n = math.prod(sizes)
    source = np.arange(n).reshape(sizes).transpose(order).reshape(-1)
    matrix = np.zeros((n, n), np.float32)
    matrix[source, np.arange(n)] = 1.0
    return matrix.astype(jnp.bfloat16)


def dot(a, b, dims=((1,), (0,))):
    return lax.dot_general(a, b, (dims, ((), ())), preferred_element_type=jnp.float32)


def in_hbm(x):
    return pltpu.with_memory_space_constraint(x, pltpu.HBM)


def receiver_kernel(
    x_hbm, table_hbm, mover_hbm, out_ref, x, table, moves, arrived, rows
):
    copies = [
        pltpu.make_async_copy(table_hbm, table, arrived.at[0]),
        pltpu.make_async_copy(x_hbm, x, arrived.at[1]),
        pltpu.make_async_copy(mover_hbm, moves, arrived.at[2]),
    ]
    for copy in copies:
        copy.start()
    copies[0].wait()
    copies[1].wait()
    spectra = dot(x[...].reshape(512, NT), table[...]).astype(jnp.bfloat16)
    copies[2].wait()
    moved = dot(spectra, moves[...], ((0,), (0,)))
    low = lax.broadcasted_iota(jnp.int32, (NF, 128), 1) < 64
    for pair in range(4):
        real = moved[:NF, pair * 128 : (pair + 1) * 128]
        imag = moved[NF:, pair * 128 : (pair + 1) * 128]
        even = jnp.where(low, real, pltpu.roll(imag, 64, 1))
        odd = jnp.where(low, pltpu.roll(real, 64, 1), imag)
        rows[pl.ds(2 * pair, NF, stride=8), :] = even
        rows[pl.ds(2 * pair + 1, NF, stride=8), :] = odd
    out_ref[...] = rows[...].astype(jnp.bfloat16)


def receiver_spectra(traces, table):
    moves = jnp.asarray(mover((32, 8, 2), (1, 2, 0)))
    return pl.pallas_call(
        receiver_kernel,
        out_shape=pltpu.VMEM((NF * 8, 128), jnp.bfloat16),
        in_specs=[HBM] * 3,
        out_specs=VMEM,
        scratch_shapes=[
            pltpu.VMEM((32, 16, NT), jnp.bfloat16),
            pltpu.VMEM((NT, 128), jnp.bfloat16),
            pltpu.VMEM((512, 512), jnp.bfloat16),
            pltpu.SemaphoreType.DMA((3,)),
            pltpu.VMEM((NF * 8, 128), jnp.float32),
        ],
        compiler_params=pltpu.CompilerParams(vmem_limit_bytes=16 << 20),
        cost_estimate=pl.CostEstimate(
            flops=200 * 512 * 128 * NT, bytes_accessed=3 << 20, transcendentals=0
        ),
        name="receiver_spectra",
    )(in_hbm(traces), in_hbm(table), in_hbm(moves))


AT_ONCE = 2


def source_kernel(x_ref, own_ref, table_ref, out_ref, rows):
    out_ref[:, 32:40, :] = own_ref[...].reshape(NF, 8, 128)

    @pl.loop(0, 8 // AT_ONCE)
    def _(step):
        first = step * AT_ONCE
        traces = x_ref[pl.ds(first, AT_ONCE)].reshape(AT_ONCE * 256, NT)
        spectra = dot(traces, table_ref[...]).T
        for j in range(AT_ONCE):
            for c in range(2):
                for kh in range(2):
                    at = j * 256 + kh * 128
                    rows[pl.ds(kh * 16 + c * 8 + first + j, NF, stride=32), :] = spectra[
                        c * NF : (c + 1) * NF, at : at + 128
                    ]

    out_ref[:, :32, :] = rows[...].astype(jnp.bfloat16).reshape(NF, 32, 128)


def source_spectra(traces, own, table):
    return pl.pallas_call(
        source_kernel,
        out_shape=jax.ShapeDtypeStruct((NF, 64, 128), jnp.bfloat16),
        in_specs=[VMEM] * 3,
        out_specs=VMEM,
        scratch_shapes=[pltpu.VMEM((NF * 32, 128), jnp.float32)],
        compiler_params=pltpu.CompilerParams(vmem_limit_bytes=8 << 20),
        cost_estimate=pl.CostEstimate(
            flops=2 * 2048 * 128 * NT, bytes_accessed=10 << 20, transcendentals=0
        ),
        name="source_spectra",
    )(traces, own, table)


def swapped(tiles):
    group = lax.broadcasted_iota(jnp.int32, tiles[0].shape, 1) // 32
    for bit in (1, 2):
        keep = (group & bit) == 0
        tiles = list(tiles)
        for i in range(4):
            if not i & bit:
                a, b = tiles[i], tiles[i + bit]
                tiles[i] = jnp.where(keep, a, pltpu.roll(b, 32 * bit, 1))
                tiles[i + bit] = jnp.where(keep, pltpu.roll(a, 128 - 32 * bit, 1), b)
    return tiles


def product_kernel(z1_ref, wave_ref, got_ref, out_ref, right, pred, rows):
    z1 = z1_ref[0]
    left, coupled = [], []
    for pair in range(2):
        at = 32 + 16 * pair
        pieces = [
            got_ref[:, row, at : at + 16, :].reshape(256, 128).astype(jnp.float32) for row in range(4)
        ]
        tiles = [tile.reshape(2, 8, 2, 8, 128) for tile in swapped(pieces)]
        for half in range(2):
            slot = 2 * pair + half
            origin = lax.rem(z1 - SLOTS[slot] + 4, 4)
            for yh in range(2):
                panel = 2 * yh + lax.div(origin, 2)
                start = pl.multiple_of(16 * lax.rem(origin, 2), 16)
                left.append(got_ref[:, panel, pl.ds(start, 16), :].reshape(256, 128))
                for k in range(2):
                    for c in range(2):
                        part = tiles[2 * c + k][yh, :, half]
                        if SLOTS[slot] == 2:
                            part = jnp.concatenate([part[4:], part[:4]], axis=0)
                        right[slot, c, pl.ds(yh * 128 + k, 64, stride=2), :] = part.reshape(64, 128)
            both = jnp.concatenate([right[slot, 0], right[slot, 1]], axis=1)
            coupled.append(both.astype(jnp.bfloat16))
    raw = dot(
        jnp.concatenate(left, axis=1),
        jnp.concatenate(coupled, axis=0),
    )
    raw = raw.reshape(16, 2, 8, 256)
    real = raw[:, 0, :, :128] - raw[:, 1, :, 128:]
    imag = raw[:, 0, :, 128:] + raw[:, 1, :, :128]
    amplitude = 1.0 / math.sqrt(K)
    wave_real, wave_imag = wave_ref[0], wave_ref[1]
    pred[0] = ((real * wave_real - imag * wave_imag) * amplitude).reshape(128, 128)
    pred[1] = ((real * wave_imag + imag * wave_real) * amplitude).reshape(128, 128)
    wide = [
        jnp.concatenate(
            [
                pred[c, pl.ds(high * 4 + low, 16, stride=8), :]
                for c in range(2)
                for high in range(2)
            ],
            axis=0,
        )
        for low in range(4)
    ]
    for row, tile in enumerate(swapped(wide)):
        for q in range(4):
            rows[pl.ds(row * 4 + q, 16, stride=16), :] = tile[q * 16 : (q + 1) * 16]
    out_ref[...] = rows[...].astype(jnp.bfloat16)


def predicted_spectra(got, z1, wavelet):
    return pl.pallas_call(
        product_kernel,
        out_shape=jax.ShapeDtypeStruct((256, 128), jnp.bfloat16),
        in_specs=[SMEM, SMEM, VMEM],
        out_specs=VMEM,
        scratch_shapes=[
            pltpu.VMEM((4, 2, 256, 128), jnp.float32),
            pltpu.VMEM((2, 128, 128), jnp.float32),
            pltpu.VMEM((256, 128), jnp.float32),
        ],
        compiler_params=pltpu.CompilerParams(vmem_limit_bytes=16 << 20),
        cost_estimate=pl.CostEstimate(flops=4 << 28, bytes_accessed=2 << 20, transcendentals=0),
        name="predicted_spectra",
    )(
        z1,
        wavelet,
        got.reshape(16, 4, 64, 128),
    )


def multiples_kernel(x_ref, table_ref, out_hbm, rows, stage, sent):
    rows[...] = x_ref[...].astype(jnp.float32)
    copies = []
    for high in range(2):
        half = rows[pl.ds(high, 128, stride=2), :].astype(jnp.bfloat16).T
        for part in range(2):
            at = 1024 * part
            stage[128 * high : 128 * high + 128, at : at + 1024] = dot(
                half, table_ref[:, at : at + 1024]
            ).astype(jnp.bfloat16)
            here = (pl.ds(128 * high, 128), pl.ds(at, 1024))
            copy = pltpu.make_async_copy(stage.at[here], out_hbm.at[here], sent.at[len(copies)])
            copy.start()
            copies.append(copy)
    for copy in copies:
        copy.wait()


def multiples(returned):
    table = jnp.asarray(tables(1.0 / math.sqrt(NF)).reshape(2 * NF, NT))
    return pl.pallas_call(
        multiples_kernel,
        out_shape=jax.ShapeDtypeStruct((256, NT), jnp.bfloat16),
        in_specs=[VMEM, VMEM],
        out_specs=HBM,
        scratch_shapes=[
            pltpu.VMEM((256, 128), jnp.float32),
            pltpu.VMEM((256, NT), jnp.bfloat16),
            pltpu.SemaphoreType.DMA((4,)),
        ],
        compiler_params=pltpu.CompilerParams(vmem_limit_bytes=16 << 20),
        cost_estimate=pl.CostEstimate(
            flops=2 * 256 * 128 * NT, bytes_accessed=2 << 20, transcendentals=0
        ),
        name="multiples",
    )(returned, table)


def moves(hop):
    return [
        (2 * z1 + z0, 2 * ((z1 + hop) % 4) + (1 - z0 if hop == 2 else z0))
        for z1 in range(4)
        for z0 in range(2)
    ]


def per_device(source_traces, receiver_traces, wavelet_inverse):
    table = jnp.asarray(tables(1.0 / math.sqrt(NT)).transpose(2, 1, 0).reshape(NT, 2 * NF))
    own = receiver_spectra(receiver_traces, table)
    others = [lax.ppermute(own, ("z1", "z0"), moves(hop)) for hop in HOPS]
    sent = source_spectra(source_traces, own, table)
    others = jnp.concatenate([other.reshape(NF, 8, 128) for other in others], axis=1)
    sent = lax.dynamic_update_slice(sent, others, (0, 40, 0))
    got = lax.all_to_all(sent, GROUP, split_axis=0, concat_axis=0, tiled=True)
    wavelet = lax.dynamic_slice_in_dim(wavelet_inverse, lax.axis_index(GROUP), 1, 0).reshape(2)
    predicted = predicted_spectra(got, lax.axis_index("z1").reshape(1), wavelet)
    returned = lax.all_to_all(
        predicted.reshape(NF, 4, 128), GROUP, split_axis=0, concat_axis=0, tiled=True
    )
    return multiples(returned.reshape(256, 128)).reshape(8, 32, NT)


def solution(mesh):
    fine = Mesh(np.asarray(mesh.devices).reshape(2, 4, 2, 4, 2, 2), AXES)
    return jax.shard_map(
        per_device,
        mesh=fine,
        in_specs=(P(AF, ROW, None), P(ROW, AF, None), P()),
        out_specs=P(AF, ROW, None),
        check_vma=False,
    )
```
